32 devices in a mesh: dp: 2 (over core), row: 4 (over y, x), col: 4 (over z).
Axes of the slice: x: 2, y: 2, z: 4, core: 2. Of those that a mesh axis runs over, the one named last changes fastest.
Arguments:
- block_input: float32 [1024, 1024], P(('dp', 'col'), 'row'), may hold values from -36 to 36
- out_cot: float32 [1024, 1024], P(('dp', 'col'), 'row'), may hold values from -6 to 6
- proj_weight: float32 [1024, 3, 1024], P('row', None, ('dp', 'col')), may hold values from -0.1875 to 0.1875
- conv_weight: float32 [3, 1024], P(None, ('dp', 'col')), may hold values from -3.5 to 3.5
- mixer_weight: float32 [1024, 1024], P(('dp', 'col'), 'row'), may hold values from -0.1875 to 0.1875
- up_weight: float32 [1024, 2, 4608], P('row', None, ('dp', 'col')), may hold values from -0.1875 to 0.1875
- down_weight: float32 [4608, 1024], P(('dp', 'col'), 'row'), may hold values from -0.09375 to 0.09375
- norm_gains: float32 [2, 1024], P(None, 'row'), may hold values from 0.25 to 1.75
- proj_moments: float32 [2, 1024, 3, 1024], P(None, 'row', None, ('dp', 'col')), may hold values from -1024 to 1024, as said below
- conv_moments: float32 [2, 3, 1024], P(None, None, ('dp', 'col')), may hold values from -1024 to 1024, as said below
- mixer_moments: float32 [2, 1024, 1024], P(None, ('dp', 'col'), 'row'), may hold values from -1024 to 1024, as said below
- up_moments: float32 [2, 1024, 2, 4608], P(None, 'row', None, ('dp', 'col')), may hold values from -1024 to 1024, as said below
- down_moments: float32 [2, 4608, 1024], P(None, ('dp', 'col'), 'row'), may hold values from -1024 to 1024, as said below
- gains_moments: float32 [2, 2, 1024], P(None, None, 'row'), may hold values from -1024 to 1024, as said below
Outputs:
- block_output: float32 [1024, 1024], P(('dp', 'col'), 'row')
- input_grad: float32 [1024, 1024], P(('dp', 'col'), 'row')
- proj_grad: float32 [1024, 3, 1024], P('row', None, ('dp', 'col'))
- conv_grad: float32 [3, 1024], P(None, ('dp', 'col'))
- mixer_grad: float32 [1024, 1024], P(('dp', 'col'), 'row')
- up_grad: float32 [1024, 2, 4608], P('row', None, ('dp', 'col'))
- down_grad: float32 [4608, 1024], P(('dp', 'col'), 'row')
- gains_grad: float32 [2, 1024], P(None, 'row')
- proj_new: float32 [1024, 3, 1024], P('row', None, ('dp', 'col'))
- conv_new: float32 [3, 1024], P(None, ('dp', 'col'))
- mixer_new: float32 [1024, 1024], P(('dp', 'col'), 'row')
- up_new: float32 [1024, 2, 4608], P('row', None, ('dp', 'col'))
- down_new: float32 [4608, 1024], P(('dp', 'col'), 'row')
- gains_new: float32 [2, 1024], P(None, 'row')
- proj_moments_new: float32 [2, 1024, 3, 1024], P(None, 'row', None, ('dp', 'col'))
- conv_moments_new: float32 [2, 3, 1024], P(None, None, ('dp', 'col'))
- mixer_moments_new: float32 [2, 1024, 1024], P(None, ('dp', 'col'), 'row')
- up_moments_new: float32 [2, 1024, 2, 4608], P(None, 'row', None, ('dp', 'col'))
- down_moments_new: float32 [2, 4608, 1024], P(None, ('dp', 'col'), 'row')
- gains_moments_new: float32 [2, 2, 1024], P(None, None, 'row')
The draws below stay inside these ranges and needn't reach their ends.
Inputs may be any that keep to these rules, and one draw needn't show every extreme that they name: `proj_moments`: index 0 of the leading dimension holds first moments, index 1 second moments, which are positive. `conv_moments`: index 0 of the leading dimension holds first moments, index 1 second moments, which are positive. `mixer_moments`: index 0 of the leading dimension holds first moments, index 1 second moments, which are positive. `up_moments`: index 0 of the leading dimension holds first moments, index 1 second moments, which are positive. `down_moments`: index 0 of the leading dimension holds first moments, index 1 second moments, which are positive. `gains_moments`: index 0 of the leading dimension holds first moments, index 1 second moments, which are positive.
All inputs are finite; a program needn't handle non-finite values.
Results may differ from the reference program's by a relative error of at most 0.012.
The reference program's roundings to bfloat16 on the way count: a program that leaves them out, or rounds other values in their place, can miss the bound.
Values may be sent and summed in bfloat16 or wider, within the bound.
A program may use at most 128 MiB of HBM per device.

```python
import math
import jax
import jax.numpy as jnp
from jax import lax

D = 1024
FF = 4608
KERNEL = 3
STEP = 4
LEN = 512
TOKENS = 1024
N_DP = 2


def draw_block_input(key, part):
    noise_key, scale_key = jax.random.split(jax.random.fold_in(key, 3))
    columns = jnp.exp(math.log(0.3) + math.log(10.0) * jnp.arange(D, dtype=jnp.float32) / (D - 1))
    noise_field = jnp.clip(jax.random.normal(noise_key, (TOKENS, D), jnp.float32), -4.0, 4.0)
    row_scale = jnp.exp(jax.random.uniform(scale_key, (TOKENS, 1), jnp.float32, math.log(0.4), math.log(2.5)))
    return noise_field * row_scale * columns[None, :]


def moment_pair(key, shape):
    first_key, second_key = jax.random.split(jax.random.fold_in(key, 11))
    spread = 0.2 * jnp.sqrt(jnp.float32(TOKENS))
    first_moment = jnp.clip(jax.random.normal(first_key, shape, jnp.float32), -3.0, 3.0) * spread
    second_moment = jnp.exp(jax.random.uniform(second_key, shape, jnp.float32, math.log(0.0004), math.log(0.004))) * jnp.float32(TOKENS)
    return jnp.stack([first_moment, second_moment])


def draw_proj_moments(key, part):
    return moment_pair(key, (D, 3, D))


def draw_conv_moments(key, part):
    return moment_pair(key, (KERNEL, D))


def draw_mixer_moments(key, part):
    return moment_pair(key, (D, D))


def draw_up_moments(key, part):
    return moment_pair(key, (D, 2, FF))


def draw_down_moments(key, part):
    return moment_pair(key, (FF, D))


def draw_gains_moments(key, part):
    return moment_pair(key, (2, D))


def block_scale(key, shape, shards, smallest, top_value):
    def one(position, blocks):
        steps = jax.random.uniform(jax.random.fold_in(jax.random.fold_in(key, 6), position), (blocks,), jnp.float32, smallest / len(shards), top_value / len(shards))
        return jnp.repeat(jnp.exp(steps), shape[position] // blocks).reshape((-1,) + (1,) * (len(shape) - position - 1))

    gain = one(*shards[0])
    for cut in shards[1:]:
        gain = gain * one(*cut)
    return gain


def normal_values(stream_key, shape, scale, most, cuts=(), kind=jnp.bfloat16):
    entries = scale * jax.random.normal(stream_key, shape, jnp.float32)
    if cuts:
        entries = entries * block_scale(stream_key, shape, cuts, -0.22, 0.18)
    return jnp.clip(entries, -most, most).astype(kind)


def setup_inputs(seed: int = 0) -> dict:
    arg_keys = jax.random.split(jax.random.key(seed), 15)
    return {
        "block_input": draw_block_input(jax.random.fold_in(arg_keys[14], 71), 0),
        "out_cot": normal_values(arg_keys[1], (TOKENS, D), 1.0, 6.0, ((0, 8), (1, 4)), jnp.float32),
        "proj_weight": normal_values(arg_keys[2], (D, 3, D), D ** -0.5, 0.1875, ((0, 4), (2, 8)), jnp.float32),
        "conv_weight": normal_values(arg_keys[3], (KERNEL, D), KERNEL ** -0.5, 3.5, ((1, 8),), jnp.float32),
        "mixer_weight": normal_values(arg_keys[4], (D, D), D ** -0.5, 0.1875, ((0, 8), (1, 4)), jnp.float32),
        "up_weight": normal_values(arg_keys[5], (D, 2, FF), D ** -0.5, 0.1875, ((0, 4), (2, 8)), jnp.float32),
        "down_weight": normal_values(arg_keys[6], (FF, D), FF ** -0.5, 0.09375, ((0, 8), (1, 4)), jnp.float32),
        "norm_gains": jnp.clip(1.0 + 0.15 * jax.random.normal(arg_keys[7], (2, D), jnp.float32), 0.25, 1.75),
        "proj_moments": draw_proj_moments(jax.random.fold_in(arg_keys[14], 71), 0),
        "conv_moments": draw_conv_moments(jax.random.fold_in(arg_keys[14], 71), 0),
        "mixer_moments": draw_mixer_moments(jax.random.fold_in(arg_keys[14], 71), 0),
        "up_moments": draw_up_moments(jax.random.fold_in(arg_keys[14], 71), 0),
        "down_moments": draw_down_moments(jax.random.fold_in(arg_keys[14], 71), 0),
        "gains_moments": draw_gains_moments(jax.random.fold_in(arg_keys[14], 71), 0),
    }


eps_norm = 1e-05
beta_first = 0.9
beta_second = 0.999
eps_adam = 1e-08
matrix_rate = 0.01
small_rate = 0.1
decay_rate = 0.1

def plain_product(left_side, right_side):
    return jnp.dot(left_side, right_side, preferred_element_type=jnp.float32)

def contract_rows(left_side, right_side):
    return lax.dot_general(left_side, right_side, (((0,), (0,)), ((), ())), preferred_element_type=jnp.float32)

def contract_cols(left_side, right_side):
    return lax.dot_general(left_side, right_side, (((1,), (1,)), ((), ())), preferred_element_type=jnp.float32)

def adam_step(parameter, gradient, moments, step_rate, decay_weight):
    first_moment = beta_first * moments[0] + (1.0 - beta_first) * gradient
    second_moment = beta_second * moments[1] + (1.0 - beta_second) * gradient * gradient
    first_hat = first_moment / (1.0 - beta_first ** STEP)
    second_hat = second_moment / (1.0 - beta_second ** STEP)
    update = first_hat / (jnp.sqrt(second_hat) + eps_adam) + decay_weight * parameter
    return (parameter - step_rate * update, jnp.stack([first_moment, second_moment]))

def reference(block_input, out_cot, proj_weight, conv_weight, mixer_weight, up_weight, down_weight, norm_gains, proj_moments, conv_moments, mixer_moments, up_moments, down_moments, gains_moments):
    proj_low = proj_weight.astype(jnp.bfloat16).reshape(D, 3 * D)
    conv_taps = lax.optimization_barrier(conv_weight.astype(jnp.bfloat16)).astype(jnp.float32)
    mixer_low = mixer_weight.astype(jnp.bfloat16)
    up_low = up_weight.astype(jnp.bfloat16).reshape(D, 2 * FF)
    down_low = down_weight.astype(jnp.bfloat16)
    gain_one = norm_gains[0]
    gain_two = norm_gains[1]
    history = KERNEL - 1
    padding = jnp.zeros((history, D), jnp.float32)

    def one_sequence(totals, inputs):
        residual, cotangent = inputs
        inverse_one = lax.rsqrt(lax.optimization_barrier(jnp.mean(residual * residual, axis=1, keepdims=True)) + eps_norm)
        normed_one = (residual * inverse_one * gain_one).astype(jnp.bfloat16)
        projected = plain_product(normed_one, proj_low)
        gate_b = projected[:, :D]
        gate_c = projected[:, D:2 * D]
        values_x = projected[:, 2 * D:]
        mixed_input = gate_b * values_x
        padded = jnp.concatenate([padding, mixed_input], axis=0)
        convolved = conv_taps[0] * padded[0:LEN]
        for offset in range(1, KERNEL):
            convolved = convolved + conv_taps[offset] * padded[offset:offset + LEN]
        gated = (gate_c * convolved).astype(jnp.bfloat16)
        residual_two = residual + plain_product(gated, mixer_low)
        inverse_two = lax.rsqrt(lax.optimization_barrier(jnp.mean(residual_two * residual_two, axis=1, keepdims=True)) + eps_norm)
        normed_two = (residual_two * inverse_two * gain_two).astype(jnp.bfloat16)
        gate_up = plain_product(normed_two, up_low)
        gate_pre = gate_up[:, :FF]
        lifted = gate_up[:, FF:]
        sigmoid_gate = jax.nn.sigmoid(gate_pre)
        swish_gate = gate_pre * sigmoid_gate
        hidden = (swish_gate * lifted).astype(jnp.bfloat16)
        output = residual_two + plain_product(hidden, down_low)
        cot_low = cotangent.astype(jnp.bfloat16)
        d_hidden = contract_cols(cot_low, down_low)
        d_gate = d_hidden * lifted * sigmoid_gate * (1.0 + gate_pre * (1.0 - sigmoid_gate))
        d_lifted = d_hidden * swish_gate
        d_gate_up = jnp.concatenate([d_gate, d_lifted], axis=1).astype(jnp.bfloat16)
        down_part = contract_rows(hidden, cot_low)
        up_part = contract_rows(normed_two, d_gate_up)
        d_normed_two = contract_cols(d_gate_up, up_low)
        scaled_two = d_normed_two * gain_two
        gain_two_part = lax.optimization_barrier(jnp.sum(d_normed_two * residual_two * inverse_two, axis=0))
        d_residual = cotangent + inverse_two * (scaled_two - residual_two * inverse_two * inverse_two * lax.optimization_barrier(jnp.mean(scaled_two * residual_two, axis=1, keepdims=True)))
        d_residual_low = d_residual.astype(jnp.bfloat16)
        d_gated = contract_cols(d_residual_low, mixer_low)
        mixer_part = contract_rows(gated, d_residual_low)
        d_convolved = d_gated * gate_c
        d_gate_c = d_gated * convolved
        extended = jnp.concatenate([d_convolved, padding], axis=0)
        d_mixed = conv_taps[history] * extended[0:LEN]
        for offset in range(1, KERNEL):
            d_mixed = d_mixed + conv_taps[history - offset] * extended[offset:offset + LEN]
        conv_part = jnp.stack([lax.optimization_barrier(jnp.sum(d_convolved * padded[offset:offset + LEN], axis=0)) for offset in range(KERNEL)])
        d_projected = jnp.concatenate([d_mixed * values_x, d_gate_c, d_mixed * gate_b], axis=1).astype(jnp.bfloat16)
        proj_part = contract_rows(normed_one, d_projected)
        d_normed_one = contract_cols(d_projected, proj_low)
        scaled_one = d_normed_one * gain_one
        gain_one_part = lax.optimization_barrier(jnp.sum(d_normed_one * residual * inverse_one, axis=0))
        d_input = d_residual + inverse_one * (scaled_one - residual * inverse_one * inverse_one * lax.optimization_barrier(jnp.mean(scaled_one * residual, axis=1, keepdims=True)))
        parts = (proj_part, conv_part, mixer_part, up_part, down_part, jnp.stack([gain_one_part, gain_two_part]))
        new_totals = tuple((total_value + part_value for total_value, part_value in zip(totals, parts)))
        return (new_totals, (output, d_input))
    zeros_init = (jnp.zeros((D, 3 * D), jnp.float32), jnp.zeros((KERNEL, D), jnp.float32), jnp.zeros((D, D), jnp.float32), jnp.zeros((D, 2 * FF), jnp.float32), jnp.zeros((FF, D), jnp.float32), jnp.zeros((2, D), jnp.float32))
    sequences = (block_input.reshape(N_DP, LEN, D), out_cot.reshape(N_DP, LEN, D))
    totals, (outputs, input_grads) = lax.scan(one_sequence, zeros_init, sequences)
    proj_grad = totals[0].reshape(D, 3, D)
    conv_grad = totals[1]
    mixer_grad = totals[2]
    up_grad = totals[3].reshape(D, 2, FF)
    down_grad = totals[4]
    gains_grad = totals[5]
    proj_new, proj_moments_new = adam_step(proj_weight, proj_grad, proj_moments, matrix_rate, decay_rate)
    conv_new, conv_moments_new = adam_step(conv_weight, conv_grad, conv_moments, small_rate, 0.0)
    mixer_new, mixer_moments_new = adam_step(mixer_weight, mixer_grad, mixer_moments, matrix_rate, decay_rate)
    up_new, up_moments_new = adam_step(up_weight, up_grad, up_moments, matrix_rate, decay_rate)
    down_new, down_moments_new = adam_step(down_weight, down_grad, down_moments, matrix_rate, decay_rate)
    gains_new, gains_moments_new = adam_step(norm_gains, gains_grad, gains_moments, small_rate, 0.0)
    return (outputs.reshape(TOKENS, D), input_grads.reshape(TOKENS, D), proj_grad, conv_grad, mixer_grad, up_grad, down_grad, gains_grad, proj_new, conv_new, mixer_new, up_new, down_new, gains_new, proj_moments_new, conv_moments_new, mixer_moments_new, up_moments_new, down_moments_new, gains_moments_new)
```

```python
import jax
import jax.numpy as jnp
from jax import lax
from jax.experimental import pallas as pl
from jax.experimental.pallas import tpu as pltpu
from jax.sharding import PartitionSpec as P

KERNEL = 3
STEP = 4
HISTORY = KERNEL - 1
RIM = 8

eps_norm = 1e-05
beta_first = 0.9
beta_second = 0.999
eps_adam = 1e-08
matrix_rate = 0.01
small_rate = 0.1
decay_rate = 0.1

LOW = jnp.bfloat16
F32 = jnp.float32
MESH = pl.DeviceIdType.MESH
VMEM_LIMIT = 60 * 1024 * 1024


def plain_product(left_side, right_side):
    return jnp.dot(left_side, right_side, preferred_element_type=F32)


def contract_rows(left_side, right_side):
    return lax.dot_general(
        left_side, right_side, (((0,), (0,)), ((), ())), preferred_element_type=F32
    )


def contract_cols(left_side, right_side):
    return lax.dot_general(
        left_side, right_side, (((1,), (1,)), ((), ())), preferred_element_type=F32
    )


def adam(parameter, gradient, first, second, step_rate, decay_weight):
    first_moment = beta_first * first + (1.0 - beta_first) * gradient
    second_moment = beta_second * second + (1.0 - beta_second) * gradient * gradient
    first_hat = first_moment / (1.0 - beta_first**STEP)
    second_hat = second_moment / (1.0 - beta_second**STEP)
    update = first_hat / (jnp.sqrt(second_hat) + eps_adam) + decay_weight * parameter
    return parameter - step_rate * update, first_moment, second_moment


def padded_rows(count):
    return -(-count // 16) * 16


class Names:
    def __init__(self, **items):
        self.items = items
        self.__dict__.update(items)

    def bound(self, refs):
        return Names(**dict(zip(self.items, refs)))


class Ring:
    def __init__(self, axis, size):
        assert size & (size - 1) == 0
        self.axis, self.size = axis, size
        self.me = lax.axis_index(axis)

    def peer(self, step):
        index, bit = jnp.int32(0), 1
        while bit < self.size:
            digit = lax.rem(lax.div(self.me, jnp.int32(bit)), jnp.int32(2))
            index = index + ((1 - digit) if step & bit else digit) * bit
            bit *= 2
        return index

    def steps(self):
        return range(1, self.size)


class Shapes:
    def __init__(self, sizes, tokens, width, channels, units):
        self.dp, self.row, self.col = sizes
        self.tokens, self.width = tokens, width
        self.rows = tokens // self.row
        self.length = tokens * self.col
        self.full = width * self.row
        self.stored_chan, self.stored_unit = channels, units
        self.cut_chan, self.cut_unit = channels // self.row, units // self.row
        self.chan = padded_rows(self.cut_chan)
        self.unit = padded_rows(self.cut_unit)
        self.chans = self.chan * self.dp
        self.units = self.unit * self.dp
        self.spots = 8 * (self.col * self.row + self.col) + 20 * self.row + 12 * self.dp + self.col


def block_kernel(s, ins, outs, tmp, send_sem, recv_sem, own_sem):
    dp, row, col = Ring("dp", s.dp), Ring("row", s.row), Ring("col", s.col)
    h, r, c = dp.me, row.me, col.me
    taken = [0]
    sent = []

    barrier = pltpu.get_barrier_semaphore()
    for ring in (row, col, dp):
        for step in ring.steps():
            pl.semaphore_signal(
                barrier, inc=1, device_id={ring.axis: ring.peer(step)}, device_id_type=MESH
            )

    here = ins.bound(tmp.arguments)
    loads = Names(
        **{
            key: pltpu.make_async_copy(source, target, own_sem.at[4 + index])
            for index, (key, source, target) in enumerate(
                zip(ins.items, ins.items.values(), tmp.arguments)
            )
        }
    )
    for copy in loads.items.values():
        copy.start()
    ins = here

    def take(count):
        taken[0] += count
        assert taken[0] <= s.spots
        return taken[0] - count

    def make(src, dst, send, recv, ring, peer):
        return pltpu.make_async_remote_copy(
            src_ref=src,
            dst_ref=dst,
            send_sem=send_sem.at[send],
            recv_sem=recv_sem.at[recv],
            device_id={ring.axis: peer},
            device_id_type=MESH,
        )

    def remote(src, dst, spot, ring, peer):
        copy = make(src, dst, spot, spot, ring, peer)
        copy.start()
        sent.append(copy)
        return copy

    def wait_all(copies):
        for copy in copies:
            copy.wait_recv()

    def span(index, size):
        return pl.ds(pl.multiple_of(index * size, size), size)

    def row_cols(index):
        return span(index, s.width)

    def block(b):
        return pl.ds(b * s.tokens, s.tokens)

    blocks = range(s.col)

    def line(b):
        return pl.ds(pl.multiple_of(b * s.tokens + r * s.rows, s.rows), s.rows)

    class Gather:
        def __init__(self, array, square):
            self.array, self.square = array, square
            self.z, self.xy = take(s.col), take(s.col * s.row)

        def piece(self, b):
            if self.square:
                return self.array.at[span(b, s.tokens), row_cols(r)]
            return self.array.at[line(b), :]

        def z_copy(self, source, target):
            part = self.piece(source)
            return make(part, part, self.z + target, self.z + source, col, target)

        def xy_copy(self, b, other):
            part = self.piece(b)
            spot = self.xy + b * s.row + other
            return make(part, part, spot, spot, row, row.peer(other))

        def start(self, b):
            @pl.when(c == b)
            def _():
                for target in blocks:
                    if target != b:
                        self.z_copy(b, target).start()
                for other in row.steps():
                    self.xy_copy(b, other).start()

        def forward(self, b):
            @pl.when(c != b)
            def _():
                self.z_copy(b, (b + 1) % s.col).wait_recv()
                for other in row.steps():
                    self.xy_copy(b, other).start()

        def wait(self, b):
            for other in row.steps():
                self.xy_copy(b, other).wait_recv()

        def finish(self):
            for b in blocks:
                for other in row.steps():
                    self.xy_copy(b, other).wait_send()

                @pl.when(c == b)
                def _(b=b):
                    for target in blocks:
                        if target != b:
                            self.z_copy(b, target).wait_send()

    class Scatter:
        def __init__(self, out, one, mid, two):
            self.out, self.one, self.mid, self.two = out, one, mid, two
            self.z, self.xy = take(s.col), take(s.col * s.row)

        def xy_copy(self, b, other):
            peer = row.peer(other)
            spot = self.xy + b * s.row + other
            return make(
                self.out.at[b, span(peer, s.rows), :], self.one.at[b, other], spot, spot, row, peer
            )

        def z_copy(self, b, source):
            return make(
                self.mid.at[b], self.two.at[source], self.z + b, self.z + source, col, b
            )

        def chunk(self, b, partial):
            self.out[b] = partial.astype(LOW)
            for other in row.steps():
                self.xy_copy(b, other).start()

        def square_sum(self, b):
            total = self.out[b, span(r, s.rows), :].astype(F32)
            for other in row.steps():
                self.xy_copy(b, other).wait_recv()
                total = total + self.one[b, other].astype(F32)
            return total

        def relay(self, b):
            @pl.when(c != b)
            def _():
                self.mid[b] = self.square_sum(b).astype(LOW)
                self.z_copy(b, c).start()

        def total(self, b):
            total = self.square_sum(b)
            for source in blocks:
                if source != b:
                    self.z_copy(b, source).wait_recv()
                    total = total + self.two[source].astype(F32)
            return total

        def finish(self):
            for b in blocks:
                for other in row.steps():
                    self.xy_copy(b, other).wait_send()

                @pl.when(c != b)
                def _(b=b):
                    self.z_copy(b, c).wait_send()

    def cut(target, values, stored, kept, padded):
        for part in range(s.row):
            lead = (slice(None),) * (len(target.shape) - 3)
            where = lead + (part,) if lead else (part,)
            if padded != kept:
                target[where + (slice(None), slice(None))] = jnp.zeros(
                    target.shape[: len(lead)] + target.shape[-2:], LOW
                )
            piece = values(part * kept, kept)
            target[where + (pl.ds(0, kept), slice(None))] = piece.astype(LOW)

    loads.proj.wait()
    for part in range(3):
        tmp.turned[part] = ins.proj[part].T
    cut(
        tmp.s_proj, lambda at, size: tmp.turned[:, at : at + size, :], 0, s.cut_chan, s.chan
    )
    loads.mixer.wait()
    cut(tmp.s_mixer, lambda at, size: ins.mixer[at : at + size, :], 0, s.cut_chan, s.chan)
    loads.up.wait()
    cut(tmp.s_up, lambda at, size: ins.up[:, at : at + size, :], 0, s.cut_unit, s.unit)
    loads.down.wait()
    cut(tmp.s_down, lambda at, size: ins.down[at : at + size, :], 0, s.cut_unit, s.unit)

    loads.x.wait()
    loads.cot.wait()
    loads.gains.wait()
    loads.taps.wait()
    tmp.x_all[span(c, s.tokens), row_cols(r)] = ins.x[...].astype(LOW)
    tmp.cot_all[span(c, s.tokens), row_cols(r)] = ins.cot[...].astype(LOW)
    tmp.gains_own[...] = jnp.zeros(tmp.gains_own.shape, F32)
    tmp.gains_own[0:2, :] = ins.gains[...]
    tmp.gains_all[:, row_cols(r)] = tmp.gains_own[...]

    def chooser(shape, stored_dim):
        here_dim = 1 - stored_dim
        stored = lax.broadcasted_iota(jnp.int32, shape, stored_dim) - r * s.cut_chan
        here = lax.broadcasted_iota(jnp.int32, shape, here_dim) - h * s.chan
        return ((stored == here) & (here >= 0) & (here < s.cut_chan)).astype(F32)

    stored_taps = jnp.concatenate(
        [ins.taps[...], jnp.zeros((8 - KERNEL, s.stored_chan), F32)], axis=0
    )
    taps = plain_product(
        stored_taps.astype(LOW), chooser((s.stored_chan, s.chans), 0).astype(LOW)
    )
    tmp.tap_own[...] = taps

    pl.semaphore_wait(barrier, s.row + s.col + s.dp - 3)

    own_copies = []

    class Weight:
        def __init__(self, source, target):
            self.lead = (slice(None),) * (len(target.shape) - 2)
            self.size = source.shape[-2]
            self.target = target
            self.spot, self.across = take(s.row), take(s.dp)
            view = target.at[self.lead + (span(h, self.size), row_cols(r))]
            self.copies = [
                remote(
                    source.at[self.lead + (row.peer(other),)],
                    view,
                    self.spot + other,
                    row,
                    row.peer(other),
                )
                for other in row.steps()
            ]
            self.own = pltpu.make_async_copy(
                source.at[self.lead + (r,)], view, own_sem.at[len(own_copies)]
            )
            self.own.start()
            own_copies.append(self.own)

        def forward(self):
            wait_all(self.copies)
            self.own.wait()
            view = self.target.at[self.lead + (span(h, self.size), slice(None))]
            self.across_copies = [
                remote(view, view, self.across + step, dp, dp.peer(step)) for step in dp.steps()
            ]

        def wait(self):
            wait_all(self.across_copies)

    class Gradient:
        def __init__(self, whole, low, land, mine, out):
            self.whole, self.low, self.land, self.mine, self.out = whole, low, land, mine, out
            self.lead = (slice(None),) * (len(whole.shape) - 2)
            self.size = whole.shape[-2] // s.dp
            self.spot, self.across = take(s.row), take(s.dp)

        def start(self, parts):
            for index, value in enumerate(parts):
                where = ((index,) if self.lead else ()) + (slice(None), slice(None))
                self.whole[where] = value
                self.low[where] = value.astype(LOW)
            self.copies = []
            for step in dp.steps():
                view = self.low.at[self.lead + (span(dp.peer(step), self.size), slice(None))]
                self.copies.append(
                    remote(view, self.land.at[step], self.across + step, dp, dp.peer(step))
                )

        def spread(self):
            total = self.whole[self.lead + (span(h, self.size), slice(None))]
            for step, copy in zip(dp.steps(), self.copies):
                copy.wait_recv()
                total = total + self.land[step].astype(F32)
            self.mine[...] = total.astype(LOW)
            keep = self.lead + (slice(None),)
            self.last = []
            for other in row.steps():
                peer = row.peer(other)
                self.last.append(
                    remote(
                        self.mine.at[keep + (row_cols(peer),)],
                        self.out.at[self.lead + (r,)],
                        self.spot + other,
                        row,
                        peer,
                    )
                )
            self.out[self.lead + (r, slice(None), slice(None))] = self.mine[keep + (row_cols(r),)]

        def wait(self):
            wait_all(self.last)

    def squares_out(target, source):
        spot = take(s.row)
        copies = [
            remote(
                source.at[:, row_cols(row.peer(other))],
                target.at[span(r, s.rows), :],
                spot + other,
                row,
                row.peer(other),
            )
            for other in row.steps()
        ]
        target[span(r, s.rows), :] = source[:, row_cols(r)]
        return copies

    def rows_in(target, source):
        spot = take(s.row)
        copies = [
            remote(
                source.at[span(row.peer(other), s.rows), :],
                target.at[:, row_cols(r)],
                spot + other,
                row,
                row.peer(other),
            )
            for other in row.steps()
        ]
        target[:, row_cols(r)] = source[span(r, s.rows), :]
        return copies

    def all_reduce(ring, source, land):
        spot = take(ring.size)
        return [
            remote(source, land.at[step], spot + step, ring, ring.peer(step))
            for step in ring.steps()
        ]

    def landed(ring, total, land, copies):
        for step, copy in zip(ring.steps(), copies):
            copy.wait_recv()
            total = total + land[step]
        return total

    first = Gather(tmp.x_all, True)
    for b in blocks:
        first.start(b)
    mine = tmp.cot_all.at[span(c, s.tokens), row_cols(r)]
    spot = take(s.row)
    cot_square = [
        remote(mine, mine, spot + other, row, row.peer(other)) for other in row.steps()
    ]
    w_proj = Weight(tmp.s_proj, tmp.w_proj)
    spot = take(s.row)
    gain_copies = [
        remote(
            tmp.gains_own, tmp.gains_all.at[:, row_cols(r)], spot + other, row, row.peer(other)
        )
        for other in row.steps()
    ]
    tap_copies = all_reduce(dp, tmp.tap_own, tmp.tap_land)
    w_mixer = Weight(tmp.s_mixer, tmp.w_mixer)
    for b in blocks:
        first.forward(b)
    wait_all(cot_square)
    mine = tmp.cot_all.at[span(c, s.tokens), :]
    spot = take(s.col)
    cot_line = [
        remote(mine, mine, spot + step, col, col.peer(step)) for step in col.steps()
    ]
    w_proj.forward()
    w_mixer.forward()
    x_rows = rows_in(tmp.x_rows, ins.x)
    wait_all(gain_copies)
    taps = landed(dp, taps, tmp.tap_land, tap_copies)
    gain_one = tmp.gains_all[0:1, :]
    gain_two = tmp.gains_all[1:2, :]
    w_proj.wait()

    scatter_mixer = Scatter(tmp.m_out, tmp.m_one, tmp.m_mid, tmp.m_two)
    parts, mixed = tmp.parts, tmp.mixed
    length = s.length
    mixed[0:RIM, :] = jnp.zeros((RIM, s.chans), F32)
    for b in blocks:
        first.wait(b)
        value = tmp.x_all[block(b), :].astype(F32)
        mean = jnp.sum(value * value, axis=1, keepdims=True) / s.full
        low = (value * lax.rsqrt(mean + eps_norm) * gain_one).astype(LOW)
        tmp.normed_one[block(b), :] = low
        for part in range(3):
            parts[part, block(b), :] = contract_cols(low, tmp.w_proj[part])
        start = RIM + b * s.tokens
        mixed[start : start + s.tokens, :] = parts[0, block(b), :] * parts[2, block(b), :]
        convolved = jnp.zeros((s.tokens, s.chans), F32)
        for offset in range(KERNEL):
            at = start - HISTORY + offset
            convolved = convolved + taps[offset : offset + 1] * mixed[at : at + s.tokens, :]
        tmp.convolved[block(b), :] = convolved
        gated = (parts[1, block(b), :] * convolved).astype(LOW)
        tmp.gated[block(b), :] = gated
        if b == 0:
            w_mixer.wait()
        scatter_mixer.chunk(b, plain_product(gated, tmp.w_mixer[...]))

    w_up = Weight(tmp.s_up, tmp.w_up)
    w_down = Weight(tmp.s_down, tmp.w_down)
    cot_rows = rows_in(tmp.cot_rows, ins.cot)

    second = Gather(tmp.two_all, False)

    def norm_two(residual):
        mean = jnp.sum(residual * residual, axis=1, keepdims=True) / s.full
        return lax.rsqrt(mean + eps_norm)

    def own_two(b):
        @pl.when(c == b)
        def _():
            total = scatter_mixer.total(b)
            wait_all(x_rows)
            residual = tmp.x_rows[...] + total
            tmp.residual_two[...] = residual
            tmp.two_all[line(b), :] = (residual * norm_two(residual) * gain_two).astype(LOW)

        second.start(b)

    scatter_two = Scatter(tmp.b_out, tmp.b_one, tmp.b_mid, tmp.b_two)

    def ffn(b):
        second.wait(b)
        value = tmp.two_all[block(b), :]
        back = contract_cols(tmp.cot_all[block(b), :], tmp.w_down[...])
        gate_pre = contract_cols(value, tmp.w_up[0])
        lifted = contract_cols(value, tmp.w_up[1])
        sigmoid_gate = jax.nn.sigmoid(gate_pre)
        swish_gate = gate_pre * sigmoid_gate
        tmp.hidden[block(b), :] = (swish_gate * lifted).astype(LOW)
        gate_low = (
            back * lifted * sigmoid_gate * (1.0 + gate_pre * (1.0 - sigmoid_gate))
        ).astype(LOW)
        lift_low = (back * swish_gate).astype(LOW)
        tmp.d_gate[block(b), :] = gate_low
        tmp.d_lift[block(b), :] = lift_low
        scatter_two.chunk(
            b, plain_product(gate_low, tmp.w_up[0]) + plain_product(lift_low, tmp.w_up[1])
        )

    third = Gather(tmp.res_all, False)
    tmp.gain_part[...] = jnp.zeros(tmp.gain_part.shape, F32)

    def own_three(b):
        @pl.when(c == b)
        def _():
            d_normed = scatter_two.total(b)
            residual = tmp.residual_two[...]
            wait_all(cot_rows)
            inverse = norm_two(residual)
            scaled = d_normed * gain_two
            row_mean = jnp.sum(scaled * residual, axis=1, keepdims=True) / s.full
            d_residual = tmp.cot_rows[...] + inverse * (
                scaled - residual * inverse * inverse * row_mean
            )
            tmp.d_residual[...] = d_residual
            tmp.res_all[line(b), :] = d_residual.astype(LOW)
            tmp.gain_part[1:2, :] = jnp.sum(d_normed * residual * inverse, axis=0, keepdims=True)

        third.start(b)

    feed_z, feed_xy = take(s.col), take(s.row)
    feed_copies = {}

    def feed(step):
        at = span(col.peer(step) if step else c, s.tokens)
        partial = plain_product(tmp.hidden[at, :], tmp.w_down[...])
        tmp.f_out[step] = partial.astype(LOW)
        if step:
            feed_copies[step] = remote(
                tmp.f_out.at[step], tmp.f_land.at[step], feed_z + step, col, col.peer(step)
            )

    def feed_spread():
        total = tmp.f_out[0].astype(F32)
        for step, copy in feed_copies.items():
            copy.wait_recv()
            total = total + tmp.f_land[step].astype(F32)
        tmp.f_mid[...] = total.astype(LOW)
        return [
            remote(
                tmp.f_mid.at[:, row_cols(row.peer(other))],
                tmp.f_last.at[other],
                feed_xy + other,
                row,
                row.peer(other),
            )
            for other in row.steps()
        ]

    def feed_out(copies):
        wait_all(res_square)
        total = tmp.f_mid[:, row_cols(r)].astype(F32)
        for other, copy in zip(row.steps(), copies):
            copy.wait_recv()
            total = total + tmp.f_last[other].astype(F32)
        outs.block_output[...] = tmp.res_square[...] + total

    g_up = Gradient(tmp.gf_up, tmp.gb_up, tmp.gl_up, tmp.gs_up, outs.g_up)
    g_down = Gradient(tmp.gf_down, tmp.gb_down, tmp.gl_down, tmp.gs_down, outs.g_down)
    g_mixer = Gradient(tmp.gf_mixer, tmp.gb_mixer, tmp.gl_mixer, tmp.gs_mixer, outs.g_mixer)
    g_proj = Gradient(tmp.gf_proj, tmp.gb_proj, tmp.gl_proj, tmp.gs_proj, outs.g_proj)
    relay = scatter_mixer.relay
    relay(0)
    relay(1)
    own_two(0)
    relay(2)
    own_two(1)
    second.forward(0)
    relay(3)
    own_two(2)
    second.forward(1)
    own_two(3)
    second.forward(2)
    w_up.forward()
    w_down.forward()
    second.forward(3)
    wait_all(cot_line)
    w_up.wait()
    w_down.wait()
    ffn(0)
    ffn(1)
    ffn(2)
    scatter_two.relay(0)
    ffn(3)
    g_up.start(
        [
            contract_rows(tmp.d_gate[...], tmp.two_all[...]),
            contract_rows(tmp.d_lift[...], tmp.two_all[...]),
        ]
    )
    g_down.start([contract_rows(tmp.hidden[...], tmp.cot_all[...])])
    scatter_two.relay(1)
    own_three(0)
    g_up.spread()
    scatter_two.relay(2)
    own_three(1)
    third.forward(0)
    scatter_two.relay(3)
    own_three(2)
    third.forward(1)
    own_three(3)
    third.forward(2)
    third.forward(3)
    feed(3)
    feed(2)
    res_square = squares_out(tmp.res_square, tmp.residual_two)

    d_conv, d_proj = tmp.d_conv, tmp.d_proj
    d_conv[length : length + RIM, :] = jnp.zeros((RIM, s.chans), F32)
    scatter_one = Scatter(tmp.i_out, tmp.i_one, tmp.i_mid, tmp.i_two)

    def gate_back(b):
        third.wait(b)
        back = contract_cols(tmp.res_all[block(b), :], tmp.w_mixer[...])
        d_conv[block(b), :] = back * parts[1, block(b), :]
        d_proj[1, block(b), :] = (back * tmp.convolved[block(b), :]).astype(LOW)

    def conv_back(b):
        start = b * s.tokens
        d_mixed = jnp.zeros((s.tokens, s.chans), F32)
        for offset in range(KERNEL):
            tap = taps[HISTORY - offset : HISTORY - offset + 1]
            d_mixed = d_mixed + tap * d_conv[start + offset : start + offset + s.tokens, :]
        d_proj[0, block(b), :] = (d_mixed * parts[2, block(b), :]).astype(LOW)
        d_proj[2, block(b), :] = (d_mixed * parts[0, block(b), :]).astype(LOW)
        partial = plain_product(d_proj[0, block(b), :], tmp.w_proj[0])
        for part in range(1, 3):
            partial = partial + plain_product(d_proj[part, block(b), :], tmp.w_proj[part])
        scatter_one.chunk(b, partial)

    gate_back(0)
    gate_back(1)
    conv_back(0)
    gate_back(2)
    conv_back(1)
    gate_back(3)
    conv_back(2)
    conv_back(3)
    g_down.spread()

    scatter_one.relay(0)
    g_proj.start([contract_rows(d_proj[part], tmp.normed_one[...]) for part in range(3)])
    tmp.conv_part[...] = jnp.zeros(tmp.conv_part.shape, F32)
    for offset in range(KERNEL):
        start = RIM - HISTORY + offset
        tmp.conv_part[offset : offset + 1, :] = jnp.sum(
            d_conv[0:length, :] * mixed[start : start + length, :], axis=0, keepdims=True
        )
    conv_copies = all_reduce(dp, tmp.conv_part, tmp.conv_land)
    scatter_one.relay(1)
    g_proj.spread()
    scatter_one.relay(2)
    g_mixer.start([contract_rows(tmp.gated[...], tmp.res_all[...])])
    scatter_one.relay(3)
    feed(1)
    feed(0)
    g_mixer.spread()
    total = landed(dp, tmp.conv_part[...], tmp.conv_land, conv_copies)
    chosen = lax.dot_general(
        total,
        chooser((s.chans, s.stored_chan), 1),
        (((1,), (0,)), ((), ())),
        precision=lax.Precision.HIGHEST,
        preferred_element_type=F32,
    )
    tmp.conv_sum[...] = chosen
    conv_copies = all_reduce(row, tmp.conv_sum, tmp.conv_last)

    for b in blocks:

        @pl.when(c == b)
        def _(b=b):
            d_normed = scatter_one.total(b)
            value = tmp.x_rows[...]
            inverse = norm_two(value)
            tmp.gain_part[0:1, :] = jnp.sum(d_normed * value * inverse, axis=0, keepdims=True)
            scaled = d_normed * gain_one
            row_mean = jnp.sum(scaled * value, axis=1, keepdims=True) / s.full
            tmp.input_rows[...] = tmp.d_residual[...] + inverse * (
                scaled - value * inverse * inverse * row_mean
            )

    spot = take(s.row)
    gain_copies = [
        remote(
            tmp.gain_part.at[:, row_cols(row.peer(other))],
            tmp.gain_land_row.at[other],
            spot + other,
            row,
            row.peer(other),
        )
        for other in row.steps()
    ]
    input_copies = squares_out(outs.input_grad, tmp.input_rows)
    total = landed(row, tmp.gain_part[:, row_cols(r)], tmp.gain_land_row, gain_copies)
    tmp.gain_sum_row[...] = total
    gain_copies = all_reduce(col, tmp.gain_sum_row, tmp.gain_land_col)
    outs.g_conv[...] = landed(row, tmp.conv_sum[...], tmp.conv_last, conv_copies)
    feed_copies_row = feed_spread()
    total = landed(col, total, tmp.gain_land_col, gain_copies)
    tmp.gain_sum_col[...] = total
    gain_copies = all_reduce(dp, tmp.gain_sum_col, tmp.gain_land_dp)
    feed_out(feed_copies_row)
    outs.g_gains[...] = landed(dp, total, tmp.gain_land_dp, gain_copies)

    for gradient in (g_proj, g_mixer, g_up, g_down):
        gradient.wait()
    wait_all(input_copies)
    for copy in sent:
        copy.wait_send()
    for collective in (first, second, third, scatter_mixer, scatter_two, scatter_one):
        collective.finish()


def run_block(s, ins):
    outs = Names(
        block_output=((s.tokens, s.width), F32),
        input_grad=((s.tokens, s.width), F32),
        g_proj=((3, s.row, s.chan, s.width), LOW),
        g_mixer=((s.row, s.chan, s.width), LOW),
        g_up=((2, s.row, s.unit, s.width), LOW),
        g_down=((s.row, s.unit, s.width), LOW),
        g_conv=((8, s.stored_chan), F32),
        g_gains=((8, s.width), F32),
    )
    line = (s.rows, s.full)
    whole = ((s.length, s.full), LOW)
    out = ((s.col, s.tokens, s.full), LOW)
    one = ((s.col, s.row) + line, LOW)
    mid = ((s.col,) + line, LOW)
    small = ((8, s.chans), F32)
    tmp = Names(
        turned=((3, s.stored_chan, s.width), F32),
        s_proj=((3, s.row, s.chan, s.width), LOW),
        s_mixer=((s.row, s.chan, s.width), LOW),
        s_up=((2, s.row, s.unit, s.width), LOW),
        s_down=((s.row, s.unit, s.width), LOW),
        gains_own=((8, s.width), F32),
        gains_all=((8, s.full), F32),
        tap_own=small,
        tap_land=((s.dp, 8, s.chans), F32),
        w_proj=((3, s.chans, s.full), LOW),
        w_mixer=((s.chans, s.full), LOW),
        w_up=((2, s.units, s.full), LOW),
        w_down=((s.units, s.full), LOW),
        x_all=whole,
        cot_all=whole,
        two_all=whole,
        res_all=whole,
        normed_one=whole,
        m_out=out,
        m_one=one,
        m_mid=mid,
        m_two=mid,
        b_out=out,
        b_one=one,
        b_mid=mid,
        b_two=mid,
        i_out=out,
        i_one=one,
        i_mid=mid,
        i_two=mid,
        f_out=out,
        f_land=out,
        f_mid=((s.tokens, s.full), LOW),
        f_last=((s.row, s.tokens, s.width), LOW),
        res_square=((s.tokens, s.width), F32),
        x_rows=(line, F32),
        cot_rows=(line, F32),
        residual_two=(line, F32),
        d_residual=(line, F32),
        input_rows=(line, F32),
        parts=((3, s.length, s.chans), F32),
        mixed=((s.length + RIM, s.chans), F32),
        convolved=((s.length, s.chans), F32),
        gated=((s.length, s.chans), LOW),
        hidden=((s.length, s.units), LOW),
        d_gate=((s.length, s.units), LOW),
        d_lift=((s.length, s.units), LOW),
        d_conv=((s.length + RIM, s.chans), F32),
        d_proj=((3, s.length, s.chans), LOW),
        conv_part=small,
        conv_land=((s.dp, 8, s.chans), F32),
        conv_sum=((8, s.stored_chan), F32),
        conv_last=((s.row, 8, s.stored_chan), F32),
        gain_part=((8, s.full), F32),
        gain_land_row=((s.row, 8, s.width), F32),
        gain_sum_row=((8, s.width), F32),
        gain_land_col=((s.col, 8, s.width), F32),
        gain_sum_col=((8, s.width), F32),
        gain_land_dp=((s.dp, 8, s.width), F32),
        gf_proj=((3, s.chans, s.full), F32),
        gb_proj=((3, s.chans, s.full), LOW),
        gl_proj=((s.dp, 3, s.chan, s.full), LOW),
        gs_proj=((3, s.chan, s.full), LOW),
        gf_mixer=((s.chans, s.full), F32),
        gb_mixer=((s.chans, s.full), LOW),
        gl_mixer=((s.dp, s.chan, s.full), LOW),
        gs_mixer=((s.chan, s.full), LOW),
        gf_up=((2, s.units, s.full), F32),
        gb_up=((2, s.units, s.full), LOW),
        gl_up=((s.dp, 2, s.unit, s.full), LOW),
        gs_up=((2, s.unit, s.full), LOW),
        gf_down=((s.units, s.full), F32),
        gb_down=((s.units, s.full), LOW),
        gl_down=((s.dp, s.unit, s.full), LOW),
        gs_down=((s.unit, s.full), LOW),
    )

    def kernel(*refs):
        n_in, n_out = len(ins.items), len(outs.items)
        scratch = tmp.bound(refs[n_in + n_out :])
        scratch.arguments = refs[-3 - n_in : -3]
        block_kernel(
            s,
            ins.bound(refs[:n_in]),
            outs.bound(refs[n_in : n_in + n_out]),
            scratch,
            *refs[-3:],
        )

    results = pl.pallas_call(
        kernel,
        out_shape=[jax.ShapeDtypeStruct(*spec) for spec in outs.items.values()],
        in_specs=[pl.BlockSpec(memory_space=pl.ANY)] * len(ins.items),
        out_specs=[pl.BlockSpec(memory_space=pltpu.VMEM)] * len(outs.items),
        scratch_shapes=[pltpu.VMEM(*spec) for spec in tmp.items.values()]
        + [pltpu.VMEM(x.shape, x.dtype) for x in ins.items.values()]
        + [
            pltpu.SemaphoreType.DMA((s.spots,)),
            pltpu.SemaphoreType.DMA((s.spots,)),
            pltpu.SemaphoreType.DMA((4 + len(ins.items),)),
        ],
        compiler_params=pltpu.CompilerParams(
            collective_id=0, has_side_effects=True, vmem_limit_bytes=VMEM_LIMIT
        ),
    )(*ins.items.values())
    return outs.bound(results)


def update_kernel(s, small, grads, outs, refs, big_in, big_out, in_sem, out_sem):
    chunks = []
    for part in range(3):
        chunks.append((0, part, slice(None), s.stored_chan))
    for index, lead, kept in ((1, 0, s.cut_chan), (2, 2, s.cut_unit), (3, 0, s.cut_unit)):
        for first in range(max(lead, 1)):
            chunks.append((index, first if lead else None, slice(None), kept))

    def views(ref, first, moments):
        where = ((slice(None),) if moments else ()) + (() if first is None else (first,))
        return ref.at[where] if where else ref

    count = len(chunks)
    reads = []
    for k, (index, first, _, _) in enumerate(chunks):
        pair = []
        for kind in range(2):
            copy = pltpu.make_async_copy(
                views(refs[kind * 4 + index], first, kind),
                views(big_in[kind * 4 + index], first, kind),
                in_sem.at[kind * count + k],
            )
            copy.start()
            pair.append(copy)
        reads.append(pair)
    writes = []

    def gradient(index, first, kept):
        source = grads[index]
        pieces = []
        for part in range(s.row):
            where = (part,) if first is None else (first, part)
            pieces.append(source[where + (pl.ds(0, kept), slice(None))].astype(F32))
        return jnp.concatenate(pieces, axis=0)

    for k, (index, first, _, kept) in enumerate(chunks):
        for copy in reads[k]:
            copy.wait()
        if index == 0:
            value = gradient(0, first, s.cut_chan).T
        else:
            value = gradient(index, first, kept)
        where = () if first is None else (first,)
        full = (slice(None), slice(None))
        weight, moments = big_in[index], big_in[4 + index]
        new, one, two = adam(
            weight[where + full],
            value,
            moments[(0,) + where + full],
            moments[(1,) + where + full],
            matrix_rate,
            decay_rate,
        )
        big_out[index][where + full] = value
        big_out[4 + index][where + full] = new
        big_out[8 + index][(0,) + where + full] = one
        big_out[8 + index][(1,) + where + full] = two
        for kind in range(3):
            copy = pltpu.make_async_copy(
                views(big_out[kind * 4 + index], first, kind == 2),
                views(outs[kind * 4 + index], first, kind == 2),
                out_sem.at[kind * count + k],
            )
            copy.start()
            writes.append(copy)

    g_conv = small.g_conv[0:KERNEL, :]
    new, one, two = adam(
        small.conv[...], g_conv, small.conv_m[:, 0, :], small.conv_m[:, 1, :], small_rate, 0.0
    )
    small.conv_grad[...] = g_conv
    small.conv_new[...] = new
    small.conv_m_new[:, 0, :] = one
    small.conv_m_new[:, 1, :] = two
    g_gains = small.g_gains[0:2, :]
    new, one, two = adam(
        small.gains[...], g_gains, small.gains_m[0], small.gains_m[1], small_rate, 0.0
    )
    small.gains_grad[...] = g_gains
    small.gains_new[...] = new
    small.gains_m_new[0] = one
    small.gains_m_new[1] = two
    small.out_one[...] = small.in_one[...]
    small.out_two[...] = small.in_two[...]
    for copy in writes:
        copy.wait()


def run_update(s, small_in, grads, weights, moments):
    small_out = Names(
        conv_grad=small_in.conv,
        conv_new=small_in.conv,
        conv_m_new=small_in.conv_m,
        gains_grad=small_in.gains,
        gains_new=small_in.gains,
        gains_m_new=small_in.gains_m,
        out_one=small_in.in_one,
        out_two=small_in.in_two,
    )
    n_small, n_out = len(small_in.items), len(small_out.items)
    count = 3 + 1 + 2 + 1
    like = [jax.ShapeDtypeStruct(x.shape, x.dtype) for x in small_out.items.values()]
    big = [jax.ShapeDtypeStruct(x.shape, F32) for x in weights + weights + moments]

    def kernel(*refs):
        refs = list(refs)

        def grab(size):
            taken = refs[:size]
            del refs[:size]
            return taken

        names_in = grab(n_small)
        g = grab(4)
        hbm = grab(8)
        names_out = grab(n_out)
        outs = grab(12)
        big_in, big_out = grab(8), grab(12)
        small = Names(
            **dict(zip(small_in.items, names_in)), **dict(zip(small_out.items, names_out))
        )
        update_kernel(s, small, g, outs, hbm, big_in, big_out, *refs)

    vmem, here = pl.BlockSpec(memory_space=pltpu.VMEM), pl.BlockSpec(memory_space=pl.ANY)
    results = pl.pallas_call(
        kernel,
        out_shape=like + big,
        in_specs=[vmem] * (n_small + 4) + [here] * 8,
        out_specs=[vmem] * n_out + [here] * 12,
        scratch_shapes=[pltpu.VMEM(x.shape, F32) for x in weights + moments]
        + [pltpu.VMEM(x.shape, F32) for x in big]
        + [pltpu.SemaphoreType.DMA((2 * count,)), pltpu.SemaphoreType.DMA((3 * count,))],
        compiler_params=pltpu.CompilerParams(vmem_limit_bytes=VMEM_LIMIT),
    )(*small_in.items.values(), *grads, *weights, *moments)
    return small_out.bound(results[:n_out]), results[n_out:]


def on_device(
    block_input,
    out_cot,
    proj_weight,
    conv_weight,
    mixer_weight,
    up_weight,
    down_weight,
    norm_gains,
    proj_moments,
    conv_moments,
    mixer_moments,
    up_moments,
    down_moments,
    gains_moments,
):
    sizes = tuple(lax.axis_size(axis) for axis in ("dp", "row", "col"))
    s = Shapes(sizes, *block_input.shape, proj_weight.shape[2], up_weight.shape[2])
    proj_turned = proj_weight.transpose(1, 0, 2)
    up_turned = up_weight.transpose(1, 2, 0)
    ins = Names(
        x=block_input,
        cot=out_cot,
        gains=norm_gains,
        taps=conv_weight,
        proj=proj_turned,
        mixer=mixer_weight,
        up=up_turned,
        down=down_weight,
    )
    out = run_block(s, ins)
    small_in = Names(
        conv=conv_weight,
        conv_m=conv_moments.transpose(1, 0, 2),
        gains=norm_gains,
        gains_m=gains_moments,
        g_conv=out.g_conv,
        g_gains=out.g_gains,
        in_one=out.block_output,
        in_two=out.input_grad,
    )
    small, big = run_update(
        s,
        small_in,
        [out.g_proj, out.g_mixer, out.g_up, out.g_down],
        [proj_turned, mixer_weight, up_turned, down_weight],
        [
            proj_moments.transpose(0, 2, 1, 3),
            mixer_moments,
            up_moments.transpose(0, 2, 3, 1),
            down_moments,
        ],
    )
    grads, news, moments = big[:4], big[4:8], big[8:]

    def weights_of(values, taps, gains):
        return (
            values[0].transpose(1, 0, 2),
            taps,
            values[1],
            values[2].transpose(2, 0, 1),
            values[3],
            gains,
        )

    return (
        (small.out_one, small.out_two)
        + weights_of(grads, small.conv_grad, small.gains_grad)
        + weights_of(news, small.conv_new, small.gains_new)
        + (
            moments[0].transpose(0, 2, 1, 3),
            small.conv_m_new.transpose(1, 0, 2),
            moments[1],
            moments[2].transpose(0, 3, 1, 2),
            moments[3],
            small.gains_m_new,
        )
    )


def solution(mesh):
    tokens = P(("dp", "col"), "row")
    by_width = P("row", None, ("dp", "col"))
    by_unit = P(("dp", "col"), "row")
    taps = P(None, ("dp", "col"))
    gains = P(None, "row")
    weights = (by_width, taps, by_unit, by_width, by_unit, gains)
    stacked = tuple(P(None, *spec) for spec in weights)
    return jax.shard_map(
        on_device,
        mesh=mesh,
        in_specs=(tokens, tokens) + weights + stacked,
        out_specs=(tokens, tokens) + weights + weights + stacked,
        check_vma=False,
    )
```

```python
import jax
import jax.numpy as jnp
from jax import lax
from jax.experimental import pallas as pl
from jax.experimental.pallas import tpu as pltpu
from jax.sharding import PartitionSpec as P

KERNEL = 3
STEP = 4
HISTORY = KERNEL - 1
RIM = 8

eps_norm = 1e-05
beta_first = 0.9
beta_second = 0.999
eps_adam = 1e-08
matrix_rate = 0.01
small_rate = 0.1
decay_rate = 0.1

LOW = jnp.bfloat16
F32 = jnp.float32
MESH = pl.DeviceIdType.MESH
VMEM_LIMIT = 60 * 1024 * 1024


def plain_product(left_side, right_side):
    return jnp.dot(left_side, right_side, preferred_element_type=F32)


def contract_rows(left_side, right_side):
    return lax.dot_general(
        left_side, right_side, (((0,), (0,)), ((), ())), preferred_element_type=F32
    )


def contract_cols(left_side, right_side):
    return lax.dot_general(
        left_side, right_side, (((1,), (1,)), ((), ())), preferred_element_type=F32
    )


def adam(parameter, gradient, first, second, step_rate, decay_weight):
    first_moment = beta_first * first + (1.0 - beta_first) * gradient
    second_moment = beta_second * second + (1.0 - beta_second) * gradient * gradient
    first_hat = first_moment / (1.0 - beta_first**STEP)
    second_hat = second_moment / (1.0 - beta_second**STEP)
    update = first_hat / (jnp.sqrt(second_hat) + eps_adam) + decay_weight * parameter
    return parameter - step_rate * update, first_moment, second_moment


def padded_rows(count):
    return -(-count // 16) * 16


class Names:
    def __init__(self, **items):
        self.items = items
        self.__dict__.update(items)

    def bound(self, refs):
        return Names(**dict(zip(self.items, refs)))


class Ring:
    def __init__(self, axis, size):
        assert size & (size - 1) == 0
        self.axis, self.size = axis, size
        self.me = lax.axis_index(axis)

    def peer(self, step):
        index, bit = jnp.int32(0), 1
        while bit < self.size:
            digit = lax.rem(lax.div(self.me, jnp.int32(bit)), jnp.int32(2))
            index = index + ((1 - digit) if step & bit else digit) * bit
            bit *= 2
        return index

    def steps(self):
        return range(1, self.size)


class Shapes:
    def __init__(self, sizes, tokens, width, channels, units):
        self.dp, self.row, self.col = sizes
        self.tokens, self.width = tokens, width
        self.rows = tokens // self.row
        self.length = tokens * self.col
        self.full = width * self.row
        self.stored_chan, self.stored_unit = channels, units
        self.cut_chan, self.cut_unit = channels // self.row, units // self.row
        self.chan = padded_rows(self.cut_chan)
        self.unit = padded_rows(self.cut_unit)
        self.chans = self.chan * self.dp
        self.units = self.unit * self.dp
        self.spots = 8 * (self.col * self.row + self.col) + 20 * self.row + 12 * self.dp + self.col


def block_kernel(s, ins, outs, tmp, send_sem, recv_sem, own_sem):
    dp, row, col = Ring("dp", s.dp), Ring("row", s.row), Ring("col", s.col)
    h, r, c = dp.me, row.me, col.me
    taken = [0]
    sent = []

    barrier = pltpu.get_barrier_semaphore()
    for ring in (row, col, dp):
        for step in ring.steps():
            pl.semaphore_signal(
                barrier, inc=1, device_id={ring.axis: ring.peer(step)}, device_id_type=MESH
            )

    here = ins.bound(tmp.arguments)
    loads = Names(
        **{
            key: pltpu.make_async_copy(source, target, own_sem.at[4 + index])
            for index, (key, source, target) in enumerate(
                zip(ins.items, ins.items.values(), tmp.arguments)
            )
        }
    )
    for copy in loads.items.values():
        copy.start()
    ins = here

    def take(count):
        taken[0] += count
        assert taken[0] <= s.spots
        return taken[0] - count

    def make(src, dst, send, recv, ring, peer):
        return pltpu.make_async_remote_copy(
            src_ref=src,
            dst_ref=dst,
            send_sem=send_sem.at[send],
            recv_sem=recv_sem.at[recv],
            device_id={ring.axis: peer},
            device_id_type=MESH,
        )

    def remote(src, dst, spot, ring, peer):
        copy = make(src, dst, spot, spot, ring, peer)
        copy.start()
        sent.append(copy)
        return copy

    def wait_all(copies):
        for copy in copies:
            copy.wait_recv()

    def span(index, size):
        return pl.ds(pl.multiple_of(index * size, size), size)

    def row_cols(index):
        return span(index, s.width)

    def block(b):
        return pl.ds(b * s.tokens, s.tokens)

    blocks = range(s.col)

    def line(b):
        return pl.ds(pl.multiple_of(b * s.tokens + r * s.rows, s.rows), s.rows)

    class Gather:
        def __init__(self, array, square):
            self.array, self.square = array, square
            self.z, self.xy = take(s.col), take(s.col * s.row)

        def piece(self, b):
            if self.square:
                return self.array.at[span(b, s.tokens), row_cols(r)]
            return self.array.at[line(b), :]

        def z_copy(self, source, target):
            part = self.piece(source)
            return make(part, part, self.z + target, self.z + source, col, target)

        def xy_copy(self, b, other):
            part = self.piece(b)
            spot = self.xy + b * s.row + other
            return make(part, part, spot, spot, row, row.peer(other))

        def start(self, b):
            @pl.when(c == b)
            def _():
                for target in blocks:
                    if target != b:
                        self.z_copy(b, target).start()
                for other in row.steps():
                    self.xy_copy(b, other).start()

        def forward(self, b):
            @pl.when(c != b)
            def _():
                self.z_copy(b, (b + 1) % s.col).wait_recv()
                for other in row.steps():
                    self.xy_copy(b, other).start()

        def wait(self, b):
            for other in row.steps():
                self.xy_copy(b, other).wait_recv()

        def finish(self):
            for b in blocks:
                for other in row.steps():
                    self.xy_copy(b, other).wait_send()

                @pl.when(c == b)
                def _(b=b):
                    for target in blocks:
                        if target != b:
                            self.z_copy(b, target).wait_send()

    class Scatter:
        def __init__(self, out, one, mid, two):
            self.out, self.one, self.mid, self.two = out, one, mid, two
            self.z, self.xy = take(s.col), take(s.col * s.row)

        def xy_copy(self, b, other):
            peer = row.peer(other)
            spot = self.xy + b * s.row + other
            return make(
                self.out.at[b, span(peer, s.rows), :], self.one.at[b, other], spot, spot, row, peer
            )

        def z_copy(self, b, source):
            return make(
                self.mid.at[b], self.two.at[source], self.z + b, self.z + source, col, b
            )

        def chunk(self, b, partial):
            self.out[b] = partial.astype(LOW)
            for other in row.steps():
                self.xy_copy(b, other).start()

        def square_sum(self, b):
            total = self.out[b, span(r, s.rows), :].astype(F32)
            for other in row.steps():
                self.xy_copy(b, other).wait_recv()
                total = total + self.one[b, other].astype(F32)
            return total

        def relay(self, b):
            @pl.when(c != b)
            def _():
                self.mid[b] = self.square_sum(b).astype(LOW)
                self.z_copy(b, c).start()

        def total(self, b):
            total = self.square_sum(b)
            for source in blocks:
                if source != b:
                    self.z_copy(b, source).wait_recv()
                    total = total + self.two[source].astype(F32)
            return total

        def finish(self):
            for b in blocks:
                for other in row.steps():
                    self.xy_copy(b, other).wait_send()

                @pl.when(c != b)
                def _(b=b):
                    self.z_copy(b, c).wait_send()

    def cut(target, values, stored, kept, padded):
        for part in range(s.row):
            lead = (slice(None),) * (len(target.shape) - 3)
            where = lead + (part,) if lead else (part,)
            if padded != kept:
                target[where + (slice(None), slice(None))] = jnp.zeros(
                    target.shape[: len(lead)] + target.shape[-2:], LOW
                )
            piece = values(part * kept, kept)
            target[where + (pl.ds(0, kept), slice(None))] = piece.astype(LOW)

    loads.proj.wait()
    for part in range(3):
        tmp.turned[part] = ins.proj[part].T
    cut(
        tmp.s_proj, lambda at, size: tmp.turned[:, at : at + size, :], 0, s.cut_chan, s.chan
    )
    loads.mixer.wait()
    cut(tmp.s_mixer, lambda at, size: ins.mixer[at : at + size, :], 0, s.cut_chan, s.chan)
    loads.up.wait()
    cut(tmp.s_up, lambda at, size: ins.up[:, at : at + size, :], 0, s.cut_unit, s.unit)
    loads.down.wait()
    cut(tmp.s_down, lambda at, size: ins.down[at : at + size, :], 0, s.cut_unit, s.unit)

    loads.x.wait()
    loads.cot.wait()
    loads.gains.wait()
    loads.taps.wait()
    tmp.x_all[span(c, s.tokens), row_cols(r)] = ins.x[...].astype(LOW)
    tmp.cot_all[span(c, s.tokens), row_cols(r)] = ins.cot[...].astype(LOW)
    tmp.gains_own[...] = jnp.zeros(tmp.gains_own.shape, F32)
    tmp.gains_own[0:2, :] = ins.gains[...]
    tmp.gains_all[:, row_cols(r)] = tmp.gains_own[...]

    def chooser(shape, stored_dim):
        here_dim = 1 - stored_dim
        stored = lax.broadcasted_iota(jnp.int32, shape, stored_dim) - r * s.cut_chan
        here = lax.broadcasted_iota(jnp.int32, shape, here_dim) - h * s.chan
        return ((stored == here) & (here >= 0) & (here < s.cut_chan)).astype(F32)

    stored_taps = jnp.concatenate(
        [ins.taps[...], jnp.zeros((8 - KERNEL, s.stored_chan), F32)], axis=0
    )
    taps = plain_product(
        stored_taps.astype(LOW), chooser((s.stored_chan, s.chans), 0).astype(LOW)
    )
    tmp.tap_own[...] = taps

    pl.semaphore_wait(barrier, s.row + s.col + s.dp - 3)

    own_copies = []

    class Weight:
        def __init__(self, source, target):
            self.lead = (slice(None),) * (len(target.shape) - 2)
            self.size = source.shape[-2]
            self.target = target
            self.spot, self.across = take(s.row), take(s.dp)
            view = target.at[self.lead + (span(h, self.size), row_cols(r))]
            self.copies = [
                remote(
                    source.at[self.lead + (row.peer(other),)],
                    view,
                    self.spot + other,
                    row,
                    row.peer(other),
                )
                for other in row.steps()
            ]
            self.own = pltpu.make_async_copy(
                source.at[self.lead + (r,)], view, own_sem.at[len(own_copies)]
            )
            self.own.start()
            own_copies.append(self.own)

        def forward(self):
            wait_all(self.copies)
            self.own.wait()
            view = self.target.at[self.lead + (span(h, self.size), slice(None))]
            self.across_copies = [
                remote(view, view, self.across + step, dp, dp.peer(step)) for step in dp.steps()
            ]

        def wait(self):
            wait_all(self.across_copies)

    class Gradient:
        def __init__(self, whole, low, land, mine, out):
            self.whole, self.low, self.land, self.mine, self.out = whole, low, land, mine, out
            self.lead = (slice(None),) * (len(whole.shape) - 2)
            self.size = whole.shape[-2] // s.dp
            self.spot, self.across = take(s.row), take(s.dp)

        def start(self, parts):
            for index, value in enumerate(parts):
                where = ((index,) if self.lead else ()) + (slice(None), slice(None))
                self.whole[where] = value
                self.low[where] = value.astype(LOW)
            self.copies = []
            for step in dp.steps():
                view = self.low.at[self.lead + (span(dp.peer(step), self.size), slice(None))]
                self.copies.append(
                    remote(view, self.land.at[step], self.across + step, dp, dp.peer(step))
                )

        def spread(self):
            total = self.whole[self.lead + (span(h, self.size), slice(None))]
            for step, copy in zip(dp.steps(), self.copies):
                copy.wait_recv()
                total = total + self.land[step].astype(F32)
            self.mine[...] = total.astype(LOW)
            keep = self.lead + (slice(None),)
            self.last = []
            for other in row.steps():
                peer = row.peer(other)
                self.last.append(
                    remote(
                        self.mine.at[keep + (row_cols(peer),)],
                        self.out.at[self.lead + (r,)],
                        self.spot + other,
                        row,
                        peer,
                    )
                )
            self.out[self.lead + (r, slice(None), slice(None))] = self.mine[keep + (row_cols(r),)]

        def wait(self):
            wait_all(self.last)

    def squares_out(target, source):
        spot = take(s.row)
        copies = [
            remote(
                source.at[:, row_cols(row.peer(other))],
                target.at[span(r, s.rows), :],
                spot + other,
                row,
                row.peer(other),
            )
            for other in row.steps()
        ]
        target[span(r, s.rows), :] = source[:, row_cols(r)]
        return copies

    def rows_in(target, source):
        spot = take(s.row)
        copies = [
            remote(
                source.at[span(row.peer(other), s.rows), :],
                target.at[:, row_cols(r)],
                spot + other,
                row,
                row.peer(other),
            )
            for other in row.steps()
        ]
        target[:, row_cols(r)] = source[span(r, s.rows), :]
        return copies

    def all_reduce(ring, source, land):
        spot = take(ring.size)
        return [
            remote(source, land.at[step], spot + step, ring, ring.peer(step))
            for step in ring.steps()
        ]

    def landed(ring, total, land, copies):
        for step, copy in zip(ring.steps(), copies):
            copy.wait_recv()
            total = total + land[step]
        return total

    first = Gather(tmp.x_all, True)
    for b in blocks:
        first.start(b)
    mine = tmp.cot_all.at[span(c, s.tokens), row_cols(r)]
    spot = take(s.row)
    cot_square = [
        remote(mine, mine, spot + other, row, row.peer(other)) for other in row.steps()
    ]
    w_proj = Weight(tmp.s_proj, tmp.w_proj)
    spot = take(s.row)
    gain_copies = [
        remote(
            tmp.gains_own, tmp.gains_all.at[:, row_cols(r)], spot + other, row, row.peer(other)
        )
        for other in row.steps()
    ]
    tap_copies = all_reduce(dp, tmp.tap_own, tmp.tap_land)
    w_mixer = Weight(tmp.s_mixer, tmp.w_mixer)
    for b in blocks:
        first.forward(b)
    wait_all(cot_square)
    cot_spot = take(s.col)

    def cot_send(step):
        mine = tmp.cot_all.at[span(c, s.tokens), :]
        return remote(mine, mine, cot_spot + step, col, col.peer(step))

    cot_line = [cot_send(step) for step in col.steps()]
    w_proj.forward()
    w_mixer.forward()
    x_rows = rows_in(tmp.x_rows, ins.x)
    wait_all(gain_copies)
    taps = landed(dp, taps, tmp.tap_land, tap_copies)
    gain_one = tmp.gains_all[0:1, :]
    gain_two = tmp.gains_all[1:2, :]
    w_proj.wait()

    scatter_mixer = Scatter(tmp.m_out, tmp.m_one, tmp.m_mid, tmp.m_two)
    parts, mixed = tmp.parts, tmp.mixed
    length = s.length
    mixed[0:RIM, :] = jnp.zeros((RIM, s.chans), F32)
    for b in blocks:
        first.wait(b)
        value = tmp.x_all[block(b), :].astype(F32)
        mean = jnp.sum(value * value, axis=1, keepdims=True) / s.full
        low = (value * lax.rsqrt(mean + eps_norm) * gain_one).astype(LOW)
        tmp.normed_one[block(b), :] = low
        for part in range(3):
            parts[part, block(b), :] = contract_cols(low, tmp.w_proj[part])
        start = RIM + b * s.tokens
        mixed[start : start + s.tokens, :] = parts[0, block(b), :] * parts[2, block(b), :]
        convolved = jnp.zeros((s.tokens, s.chans), F32)
        for offset in range(KERNEL):
            at = start - HISTORY + offset
            convolved = convolved + taps[offset : offset + 1] * mixed[at : at + s.tokens, :]
        tmp.convolved[block(b), :] = convolved
        gated = (parts[1, block(b), :] * convolved).astype(LOW)
        tmp.gated[block(b), :] = gated
        if b == 0:
            w_mixer.wait()
        scatter_mixer.chunk(b, plain_product(gated, tmp.w_mixer[...]))

    w_up = Weight(tmp.s_up, tmp.w_up)
    w_down = Weight(tmp.s_down, tmp.w_down)
    cot_rows = rows_in(tmp.cot_rows, ins.cot)

    second = Gather(tmp.two_all, False)

    def norm_two(residual):
        mean = jnp.sum(residual * residual, axis=1, keepdims=True) / s.full
        return lax.rsqrt(mean + eps_norm)

    def own_two(b):
        @pl.when(c == b)
        def _():
            total = scatter_mixer.total(b)
            wait_all(x_rows)
            residual = tmp.x_rows[...] + total
            tmp.residual_two[...] = residual
            tmp.two_all[line(b), :] = (residual * norm_two(residual) * gain_two).astype(LOW)

        second.start(b)

    scatter_two = Scatter(tmp.b_out, tmp.b_one, tmp.b_mid, tmp.b_two)

    def ffn(b):
        second.wait(b)
        value = tmp.two_all[block(b), :]
        back = contract_cols(tmp.cot_all[block(b), :], tmp.w_down[...])
        gate_pre = contract_cols(value, tmp.w_up[0])
        lifted = contract_cols(value, tmp.w_up[1])
        sigmoid_gate = jax.nn.sigmoid(gate_pre)
        swish_gate = gate_pre * sigmoid_gate
        tmp.hidden[block(b), :] = (swish_gate * lifted).astype(LOW)
        gate_low = (
            back * lifted * sigmoid_gate * (1.0 + gate_pre * (1.0 - sigmoid_gate))
        ).astype(LOW)
        lift_low = (back * swish_gate).astype(LOW)
        tmp.d_gate[block(b), :] = gate_low
        tmp.d_lift[block(b), :] = lift_low
        scatter_two.chunk(
            b, plain_product(gate_low, tmp.w_up[0]) + plain_product(lift_low, tmp.w_up[1])
        )

    third = Gather(tmp.res_all, False)
    tmp.gain_part[...] = jnp.zeros(tmp.gain_part.shape, F32)

    def own_three(b):
        @pl.when(c == b)
        def _():
            d_normed = scatter_two.total(b)
            residual = tmp.residual_two[...]
            wait_all(cot_rows)
            inverse = norm_two(residual)
            scaled = d_normed * gain_two
            row_mean = jnp.sum(scaled * residual, axis=1, keepdims=True) / s.full
            d_residual = tmp.cot_rows[...] + inverse * (
                scaled - residual * inverse * inverse * row_mean
            )
            tmp.d_residual[...] = d_residual
            tmp.res_all[line(b), :] = d_residual.astype(LOW)
            tmp.gain_part[1:2, :] = jnp.sum(d_normed * residual * inverse, axis=0, keepdims=True)

        third.start(b)

    feed_z, feed_xy = take(s.col), take(s.row)
    feed_copies = {}

    def feed(step):
        at = span(col.peer(step) if step else c, s.tokens)
        partial = plain_product(tmp.hidden[at, :], tmp.w_down[...])
        tmp.f_out[step] = partial.astype(LOW)
        if step:
            feed_copies[step] = remote(
                tmp.f_out.at[step], tmp.f_land.at[step], feed_z + step, col, col.peer(step)
            )

    def feed_spread():
        total = tmp.f_out[0].astype(F32)
        for step, copy in feed_copies.items():
            copy.wait_recv()
            total = total + tmp.f_land[step].astype(F32)
        tmp.f_mid[...] = total.astype(LOW)
        return [
            remote(
                tmp.f_mid.at[:, row_cols(row.peer(other))],
                tmp.f_last.at[other],
                feed_xy + other,
                row,
                row.peer(other),
            )
            for other in row.steps()
        ]

    def feed_out(copies):
        wait_all(res_square)
        total = tmp.f_mid[:, row_cols(r)].astype(F32)
        for other, copy in zip(row.steps(), copies):
            copy.wait_recv()
            total = total + tmp.f_last[other].astype(F32)
        outs.block_output[...] = tmp.res_square[...] + total

    g_up = Gradient(tmp.gf_up, tmp.gb_up, tmp.gl_up, tmp.gs_up, outs.g_up)
    g_down = Gradient(tmp.gf_down, tmp.gb_down, tmp.gl_down, tmp.gs_down, outs.g_down)
    g_mixer = Gradient(tmp.gf_mixer, tmp.gb_mixer, tmp.gl_mixer, tmp.gs_mixer, outs.g_mixer)
    g_proj = Gradient(tmp.gf_proj, tmp.gb_proj, tmp.gl_proj, tmp.gs_proj, outs.g_proj)
    for b in blocks:
        scatter_mixer.relay(b)
    for b in blocks:
        own_two(b)
    for b in blocks:
        second.forward(b)
    w_down.forward()
    w_up.forward()
    wait_all(cot_line)
    w_down.wait()
    w_up.wait()
    for b in blocks:
        ffn(b)
    scatter_two.relay(0)
    g_up.start(
        [
            contract_rows(tmp.d_gate[...], tmp.two_all[...]),
            contract_rows(tmp.d_lift[...], tmp.two_all[...]),
        ]
    )
    g_down.start([contract_rows(tmp.hidden[...], tmp.cot_all[...])])
    for b in range(1, s.col):
        scatter_two.relay(b)
    for b in blocks:
        own_three(b)
    g_up.spread()
    for b in blocks:
        third.forward(b)
    for step in range(s.col - 1, 1, -1):
        feed(step)
    res_square = squares_out(tmp.res_square, tmp.residual_two)

    d_conv, d_proj = tmp.d_conv, tmp.d_proj
    d_conv[length : length + RIM, :] = jnp.zeros((RIM, s.chans), F32)
    scatter_one = Scatter(tmp.i_out, tmp.i_one, tmp.i_mid, tmp.i_two)

    def gate_back(b):
        third.wait(b)
        back = contract_cols(tmp.res_all[block(b), :], tmp.w_mixer[...])
        d_conv[block(b), :] = back * parts[1, block(b), :]
        d_proj[1, block(b), :] = (back * tmp.convolved[block(b), :]).astype(LOW)

    def conv_back(b):
        start = b * s.tokens
        d_mixed = jnp.zeros((s.tokens, s.chans), F32)
        for offset in range(KERNEL):
            tap = taps[HISTORY - offset : HISTORY - offset + 1]
            d_mixed = d_mixed + tap * d_conv[start + offset : start + offset + s.tokens, :]
        d_proj[0, block(b), :] = (d_mixed * parts[2, block(b), :]).astype(LOW)
        d_proj[2, block(b), :] = (d_mixed * parts[0, block(b), :]).astype(LOW)
        partial = plain_product(d_proj[0, block(b), :], tmp.w_proj[0])
        for part in range(1, 3):
            partial = partial + plain_product(d_proj[part, block(b), :], tmp.w_proj[part])
        scatter_one.chunk(b, partial)
        normed = tmp.normed_one[block(b), :].astype(F32)
        tmp.gain_part[0:1, :] += jnp.sum(partial * normed, axis=0, keepdims=True) / gain_one

    gate_back(0)
    for b in range(1, s.col):
        gate_back(b)
        conv_back(b - 1)
    conv_back(s.col - 1)
    spot = take(s.row)
    gain_copies = [
        remote(
            tmp.gain_part.at[:, row_cols(row.peer(other))],
            tmp.gain_land_row.at[other],
            spot + other,
            row,
            row.peer(other),
        )
        for other in row.steps()
    ]
    g_down.spread()

    scatter_one.relay(0)
    g_proj.start([contract_rows(d_proj[part], tmp.normed_one[...]) for part in range(3)])
    tmp.conv_part[...] = jnp.zeros(tmp.conv_part.shape, F32)
    for offset in range(KERNEL):
        start = RIM - HISTORY + offset
        tmp.conv_part[offset : offset + 1, :] = jnp.sum(
            d_conv[0:length, :] * mixed[start : start + length, :], axis=0, keepdims=True
        )
    conv_copies = all_reduce(dp, tmp.conv_part, tmp.conv_land)
    scatter_one.relay(1)
    g_proj.spread()
    for b in range(2, s.col - 1):
        scatter_one.relay(b)
    g_mixer.start([contract_rows(tmp.gated[...], tmp.res_all[...])])
    scatter_one.relay(s.col - 1)
    gain_total = landed(row, tmp.gain_part[:, row_cols(r)], tmp.gain_land_row, gain_copies)
    tmp.gain_sum_row[...] = gain_total
    gain_copies = all_reduce(col, tmp.gain_sum_row, tmp.gain_land_col)
    feed(1)
    feed(0)
    g_mixer.spread()
    total = landed(dp, tmp.conv_part[...], tmp.conv_land, conv_copies)
    chosen = lax.dot_general(
        total,
        chooser((s.chans, s.stored_chan), 1),
        (((1,), (0,)), ((), ())),
        precision=lax.Precision.HIGHEST,
        preferred_element_type=F32,
    )
    tmp.conv_sum[...] = chosen
    conv_copies = all_reduce(row, tmp.conv_sum, tmp.conv_last)

    for b in blocks:

        @pl.when(c == b)
        def _(b=b):
            d_normed = scatter_one.total(b)
            value = tmp.x_rows[...]
            inverse = norm_two(value)
            scaled = d_normed * gain_one
            row_mean = jnp.sum(scaled * value, axis=1, keepdims=True) / s.full
            tmp.input_rows[...] = tmp.d_residual[...] + inverse * (
                scaled - value * inverse * inverse * row_mean
            )

    input_copies = squares_out(outs.input_grad, tmp.input_rows)
    outs.g_conv[...] = landed(row, tmp.conv_sum[...], tmp.conv_last, conv_copies)
    feed_copies_row = feed_spread()
    total = landed(col, gain_total, tmp.gain_land_col, gain_copies)
    tmp.gain_sum_col[...] = total
    gain_copies = all_reduce(dp, tmp.gain_sum_col, tmp.gain_land_dp)
    feed_out(feed_copies_row)
    outs.g_gains[...] = landed(dp, total, tmp.gain_land_dp, gain_copies)

    for gradient in (g_proj, g_mixer, g_up, g_down):
        gradient.wait()
    wait_all(input_copies)
    for copy in sent:
        copy.wait_send()
    for collective in (first, second, third, scatter_mixer, scatter_two, scatter_one):
        collective.finish()


def run_block(s, ins):
    outs = Names(
        block_output=((s.tokens, s.width), F32),
        input_grad=((s.tokens, s.width), F32),
        g_proj=((3, s.row, s.chan, s.width), LOW),
        g_mixer=((s.row, s.chan, s.width), LOW),
        g_up=((2, s.row, s.unit, s.width), LOW),
        g_down=((s.row, s.unit, s.width), LOW),
        g_conv=((8, s.stored_chan), F32),
        g_gains=((8, s.width), F32),
    )
    line = (s.rows, s.full)
    whole = ((s.length, s.full), LOW)
    out = ((s.col, s.tokens, s.full), LOW)
    one = ((s.col, s.row) + line, LOW)
    mid = ((s.col,) + line, LOW)
    small = ((8, s.chans), F32)
    tmp = Names(
        turned=((3, s.stored_chan, s.width), F32),
        s_proj=((3, s.row, s.chan, s.width), LOW),
        s_mixer=((s.row, s.chan, s.width), LOW),
        s_up=((2, s.row, s.unit, s.width), LOW),
        s_down=((s.row, s.unit, s.width), LOW),
        gains_own=((8, s.width), F32),
        gains_all=((8, s.full), F32),
        tap_own=small,
        tap_land=((s.dp, 8, s.chans), F32),
        w_proj=((3, s.chans, s.full), LOW),
        w_mixer=((s.chans, s.full), LOW),
        w_up=((2, s.units, s.full), LOW),
        w_down=((s.units, s.full), LOW),
        x_all=whole,
        cot_all=whole,
        two_all=whole,
        res_all=whole,
        normed_one=whole,
        m_out=out,
        m_one=one,
        m_mid=mid,
        m_two=mid,
        b_out=out,
        b_one=one,
        b_mid=mid,
        b_two=mid,
        i_out=out,
        i_one=one,
        i_mid=mid,
        i_two=mid,
        f_out=out,
        f_land=out,
        f_mid=((s.tokens, s.full), LOW),
        f_last=((s.row, s.tokens, s.width), LOW),
        res_square=((s.tokens, s.width), F32),
        x_rows=(line, F32),
        cot_rows=(line, F32),
        residual_two=(line, F32),
        d_residual=(line, F32),
        input_rows=(line, F32),
        parts=((3, s.length, s.chans), F32),
        mixed=((s.length + RIM, s.chans), F32),
        convolved=((s.length, s.chans), F32),
        gated=((s.length, s.chans), LOW),
        hidden=((s.length, s.units), LOW),
        d_gate=((s.length, s.units), LOW),
        d_lift=((s.length, s.units), LOW),
        d_conv=((s.length + RIM, s.chans), F32),
        d_proj=((3, s.length, s.chans), LOW),
        conv_part=small,
        conv_land=((s.dp, 8, s.chans), F32),
        conv_sum=((8, s.stored_chan), F32),
        conv_last=((s.row, 8, s.stored_chan), F32),
        gain_part=((8, s.full), F32),
        gain_land_row=((s.row, 8, s.width), F32),
        gain_sum_row=((8, s.width), F32),
        gain_land_col=((s.col, 8, s.width), F32),
        gain_sum_col=((8, s.width), F32),
        gain_land_dp=((s.dp, 8, s.width), F32),
        gf_proj=((3, s.chans, s.full), F32),
        gb_proj=((3, s.chans, s.full), LOW),
        gl_proj=((s.dp, 3, s.chan, s.full), LOW),
        gs_proj=((3, s.chan, s.full), LOW),
        gf_mixer=((s.chans, s.full), F32),
        gb_mixer=((s.chans, s.full), LOW),
        gl_mixer=((s.dp, s.chan, s.full), LOW),
        gs_mixer=((s.chan, s.full), LOW),
        gf_up=((2, s.units, s.full), F32),
        gb_up=((2, s.units, s.full), LOW),
        gl_up=((s.dp, 2, s.unit, s.full), LOW),
        gs_up=((2, s.unit, s.full), LOW),
        gf_down=((s.units, s.full), F32),
        gb_down=((s.units, s.full), LOW),
        gl_down=((s.dp, s.unit, s.full), LOW),
        gs_down=((s.unit, s.full), LOW),
    )

    def kernel(*refs):
        n_in, n_out = len(ins.items), len(outs.items)
        scratch = tmp.bound(refs[n_in + n_out :])
        scratch.arguments = refs[-3 - n_in : -3]
        block_kernel(
            s,
            ins.bound(refs[:n_in]),
            outs.bound(refs[n_in : n_in + n_out]),
            scratch,
            *refs[-3:],
        )

    results = pl.pallas_call(
        kernel,
        out_shape=[jax.ShapeDtypeStruct(*spec) for spec in outs.items.values()],
        in_specs=[pl.BlockSpec(memory_space=pl.ANY)] * len(ins.items),
        out_specs=[pl.BlockSpec(memory_space=pltpu.VMEM)] * len(outs.items),
        scratch_shapes=[pltpu.VMEM(*spec) for spec in tmp.items.values()]
        + [pltpu.VMEM(x.shape, x.dtype) for x in ins.items.values()]
        + [
            pltpu.SemaphoreType.DMA((s.spots,)),
            pltpu.SemaphoreType.DMA((s.spots,)),
            pltpu.SemaphoreType.DMA((4 + len(ins.items),)),
        ],
        compiler_params=pltpu.CompilerParams(
            collective_id=0, has_side_effects=True, vmem_limit_bytes=VMEM_LIMIT
        ),
    )(*ins.items.values())
    return outs.bound(results)


def update_kernel(s, small, grads, outs, refs, big_in, big_out, in_sem, out_sem):
    chunks = []
    for part in range(3):
        chunks.append((0, part, slice(None), s.stored_chan))
    for index, lead, kept in ((1, 0, s.cut_chan), (2, 2, s.cut_unit), (3, 0, s.cut_unit)):
        for first in range(max(lead, 1)):
            chunks.append((index, first if lead else None, slice(None), kept))

    def views(ref, first, moments):
        where = ((slice(None),) if moments else ()) + (() if first is None else (first,))
        return ref.at[where] if where else ref

    count = len(chunks)
    reads = []
    for k, (index, first, _, _) in enumerate(chunks):
        pair = []
        for kind in range(2):
            copy = pltpu.make_async_copy(
                views(refs[kind * 4 + index], first, kind),
                views(big_in[kind * 4 + index], first, kind),
                in_sem.at[kind * count + k],
            )
            copy.start()
            pair.append(copy)
        reads.append(pair)
    writes = []

    def gradient(index, first, kept):
        source = grads[index]
        pieces = []
        for part in range(s.row):
            where = (part,) if first is None else (first, part)
            pieces.append(source[where + (pl.ds(0, kept), slice(None))].astype(F32))
        return jnp.concatenate(pieces, axis=0)

    for k, (index, first, _, kept) in enumerate(chunks):
        for copy in reads[k]:
            copy.wait()
        if index == 0:
            value = gradient(0, first, s.cut_chan).T
        else:
            value = gradient(index, first, kept)
        where = () if first is None else (first,)
        full = (slice(None), slice(None))
        weight, moments = big_in[index], big_in[4 + index]
        new, one, two = adam(
            weight[where + full],
            value,
            moments[(0,) + where + full],
            moments[(1,) + where + full],
            matrix_rate,
            decay_rate,
        )
        big_out[index][where + full] = value
        big_out[4 + index][where + full] = new
        big_out[8 + index][(0,) + where + full] = one
        big_out[8 + index][(1,) + where + full] = two
        for kind in range(3):
            copy = pltpu.make_async_copy(
                views(big_out[kind * 4 + index], first, kind == 2),
                views(outs[kind * 4 + index], first, kind == 2),
                out_sem.at[kind * count + k],
            )
            copy.start()
            writes.append(copy)

    g_conv = small.g_conv[0:KERNEL, :]
    new, one, two = adam(
        small.conv[...], g_conv, small.conv_m[:, 0, :], small.conv_m[:, 1, :], small_rate, 0.0
    )
    small.conv_grad[...] = g_conv
    small.conv_new[...] = new
    small.conv_m_new[:, 0, :] = one
    small.conv_m_new[:, 1, :] = two
    g_gains = small.g_gains[0:2, :]
    new, one, two = adam(
        small.gains[...], g_gains, small.gains_m[0], small.gains_m[1], small_rate, 0.0
    )
    small.gains_grad[...] = g_gains
    small.gains_new[...] = new
    small.gains_m_new[0] = one
    small.gains_m_new[1] = two
    small.out_one[...] = small.in_one[...]
    small.out_two[...] = small.in_two[...]
    for copy in writes:
        copy.wait()


def run_update(s, small_in, grads, weights, moments):
    small_out = Names(
        conv_grad=small_in.conv,
        conv_new=small_in.conv,
        conv_m_new=small_in.conv_m,
        gains_grad=small_in.gains,
        gains_new=small_in.gains,
        gains_m_new=small_in.gains_m,
        out_one=small_in.in_one,
        out_two=small_in.in_two,
    )
    n_small, n_out = len(small_in.items), len(small_out.items)
    count = 3 + 1 + 2 + 1
    like = [jax.ShapeDtypeStruct(x.shape, x.dtype) for x in small_out.items.values()]
    big = [jax.ShapeDtypeStruct(x.shape, F32) for x in weights + weights + moments]

    def kernel(*refs):
        refs = list(refs)

        def grab(size):
            taken = refs[:size]
            del refs[:size]
            return taken

        names_in = grab(n_small)
        g = grab(4)
        hbm = grab(8)
        names_out = grab(n_out)
        outs = grab(12)
        big_in, big_out = grab(8), grab(12)
        small = Names(
            **dict(zip(small_in.items, names_in)), **dict(zip(small_out.items, names_out))
        )
        update_kernel(s, small, g, outs, hbm, big_in, big_out, *refs)

    vmem, here = pl.BlockSpec(memory_space=pltpu.VMEM), pl.BlockSpec(memory_space=pl.ANY)
    results = pl.pallas_call(
        kernel,
        out_shape=like + big,
        in_specs=[vmem] * (n_small + 4) + [here] * 8,
        out_specs=[vmem] * n_out + [here] * 12,
        scratch_shapes=[pltpu.VMEM(x.shape, F32) for x in weights + moments]
        + [pltpu.VMEM(x.shape, F32) for x in big]
        + [pltpu.SemaphoreType.DMA((2 * count,)), pltpu.SemaphoreType.DMA((3 * count,))],
        compiler_params=pltpu.CompilerParams(vmem_limit_bytes=VMEM_LIMIT),
    )(*small_in.items.values(), *grads, *weights, *moments)
    return small_out.bound(results[:n_out]), results[n_out:]


def on_device(
    block_input,
    out_cot,
    proj_weight,
    conv_weight,
    mixer_weight,
    up_weight,
    down_weight,
    norm_gains,
    proj_moments,
    conv_moments,
    mixer_moments,
    up_moments,
    down_moments,
    gains_moments,
):
    sizes = tuple(lax.axis_size(axis) for axis in ("dp", "row", "col"))
    s = Shapes(sizes, *block_input.shape, proj_weight.shape[2], up_weight.shape[2])
    proj_turned = proj_weight.transpose(1, 0, 2)
    up_turned = up_weight.transpose(1, 2, 0)
    ins = Names(
        x=block_input,
        cot=out_cot,
        gains=norm_gains,
        taps=conv_weight,
        proj=proj_turned,
        mixer=mixer_weight,
        up=up_turned,
        down=down_weight,
    )
    out = run_block(s, ins)
    small_in = Names(
        conv=conv_weight,
        conv_m=conv_moments.transpose(1, 0, 2),
        gains=norm_gains,
        gains_m=gains_moments,
        g_conv=out.g_conv,
        g_gains=out.g_gains,
        in_one=out.block_output,
        in_two=out.input_grad,
    )
    small, big = run_update(
        s,
        small_in,
        [out.g_proj, out.g_mixer, out.g_up, out.g_down],
        [proj_turned, mixer_weight, up_turned, down_weight],
        [
            proj_moments.transpose(0, 2, 1, 3),
            mixer_moments,
            up_moments.transpose(0, 2, 3, 1),
            down_moments,
        ],
    )
    grads, news, moments = big[:4], big[4:8], big[8:]

    def weights_of(values, taps, gains):
        return (
            values[0].transpose(1, 0, 2),
            taps,
            values[1],
            values[2].transpose(2, 0, 1),
            values[3],
            gains,
        )

    return (
        (small.out_one, small.out_two)
        + weights_of(grads, small.conv_grad, small.gains_grad)
        + weights_of(news, small.conv_new, small.gains_new)
        + (
            moments[0].transpose(0, 2, 1, 3),
            small.conv_m_new.transpose(1, 0, 2),
            moments[1],
            moments[2].transpose(0, 3, 1, 2),
            moments[3],
            small.gains_m_new,
        )
    )


def solution(mesh):
    tokens = P(("dp", "col"), "row")
    by_width = P("row", None, ("dp", "col"))
    by_unit = P(("dp", "col"), "row")
    taps = P(None, ("dp", "col"))
    gains = P(None, "row")
    weights = (by_width, taps, by_unit, by_width, by_unit, gains)
    stacked = tuple(P(None, *spec) for spec in weights)
    return jax.shard_map(
        on_device,
        mesh=mesh,
        in_specs=(tokens, tokens) + weights + stacked,
        out_specs=(tokens, tokens) + weights + weights + stacked,
        check_vma=False,
    )
```
